32 devices in a mesh: req: 2 (over y), ctx: 16 (over z, x, core).
Axes of the slice: x: 2, y: 2, z: 4, core: 2. Of those that a mesh axis runs over, the one named last changes fastest.
Arguments:
- q_latent: bfloat16 [128, 48, 512], P(None, 'req'), parts along dimension 1, may hold values from -64 to 64
- q_rope: bfloat16 [128, 3072], P(None, 'req'), parts along dimension 1, may hold values from -6 to 6
- cache_latent: bfloat16 [128, 128, 512], P(('req', 'ctx')), parts along dimension 0, may hold values from -6 to 6
- cache_rope: bfloat16 [128, 64, 128], P(('req', 'ctx')), parts along dimension 0, may hold values from -6 to 6
- new_latent: bfloat16 [48, 512], P('req'), parts along dimension 0, may hold values from -6 to 6
- new_rope: bfloat16 [48, 64], P('req'), parts along dimension 0, may hold values from -6 to 6
- removed: int32 [24, 2], P('req'), parts along dimension 0, may hold values from 1 to 63, as said below
Outputs:
- attended: bfloat16 [128, 48, 512], P('ctx', 'req'), parts along dimension 1
The draws below stay inside these ranges and needn't reach their ends.
There are 2 independent parts, one for each index of `req`. The reference program is written for one: setup_inputs(seed, part) draws one part's arguments, and reference() takes and returns one part's arrays. A program takes and returns all parts, laid end to end along the dimension named above; each array names one. Nothing has to cross between parts.
Inputs may be any that keep to these rules, and one draw needn't show every extreme that they name: Each row (first, last) names the blocks first to last - 1 of one removed span of whole blocks. Rows ascend, the spans are disjoint and are parted by at least one kept block; the first span starts at block 1 and the last ends at block 63.
All inputs are finite; a program needn't handle non-finite values.
Results may differ from the reference program's by a relative error of at most 0.0024.
Values may be sent and summed in bfloat16 or wider, within the bound.
No kernel may reach another device: no remote copies, remote signals or barrier semaphores. Data moves between devices by JAX's collectives and lax.ppermute only.
A program may use at most 64 MiB of HBM per device.

```python
import jax
import jax.numpy as jnp
import numpy as np
from jax import lax

H = 128
LAT = 512
ROPE = 64
BLK = 128
NEW = 24
SPANS = 12
NBLK = 64
CTX = 8192


def shared_values(key):
    cache_seed = jax.random.fold_in(key, 11)
    fresh_seed = jax.random.fold_in(key, 12)
    query_seed = jax.random.fold_in(key, 13)
    strength_seed = jax.random.fold_in(key, 14)
    cache_values = jnp.clip(jax.random.normal(cache_seed, (NBLK, BLK, LAT), jnp.float32), -6.0, 6.0)
    cache_values = cache_values.astype(jnp.bfloat16).astype(jnp.float32)
    fresh_values = jnp.clip(jax.random.normal(fresh_seed, (NEW, LAT), jnp.float32), -6.0, 6.0)
    fresh_values = fresh_values.astype(jnp.bfloat16).astype(jnp.float32)
    widening = 512.0 / LAT
    strength = jnp.exp(jax.random.uniform(strength_seed, (H,), jnp.float32, jnp.log(0.1), jnp.log(0.4)))
    noise_part = jnp.clip(jax.random.normal(query_seed, (H, NEW, LAT), jnp.float32), -6.0, 6.0) * 1.5 * jnp.sqrt(widening)
    queries = noise_part + strength[:, None, None] * fresh_values[None, :, :]
    return (cache_values, fresh_values, queries)


def draw_q_latent(key, part):
    cache_values, fresh_values, queries = shared_values(key)
    return jnp.clip(queries, -64.0, 64.0).astype(jnp.bfloat16)


def draw_cache_latent(key, part):
    return shared_values(key)[0].astype(jnp.bfloat16)


def draw_new_latent(key, part):
    return shared_values(key)[1].astype(jnp.bfloat16)


def draw_removed(key, part):
    interior = jax.random.permutation(jax.random.fold_in(key, 21), NBLK - 3)[:2 * SPANS - 2] + 2
    bounds = jnp.sort(jnp.concatenate([jnp.array([1, NBLK - 1], jnp.int32), interior.astype(jnp.int32)]))
    return bounds.reshape(SPANS, 2)


def block_levels(key, shape, pieces, least, top_value):
    def one(position, parts):
        heights = jax.random.uniform(jax.random.fold_in(jax.random.fold_in(key, 6), position), (parts,), jnp.float32, least / len(pieces), top_value / len(pieces))
        return jnp.repeat(jnp.exp(heights), shape[position] // parts).reshape((-1,) + (1,) * (len(shape) - position - 1))

    factor_of = one(*pieces[0])
    for cut in pieces[1:]:
        factor_of = factor_of * one(*cut)
    return factor_of


def noise(rng, dims, scale, limit, pieces=(), held_as=jnp.bfloat16):
    values = scale * jax.random.normal(rng, dims, jnp.float32)
    if pieces:
        values = values * block_levels(rng, dims, pieces, -0.22, 0.18)
    return jnp.clip(values, -limit, limit).astype(held_as)


def setup_inputs(seed: int = 0, part: int = 0) -> dict:
    key_of = jax.random.split(jax.random.key(seed), 8)
    own_keys = jax.random.split(jax.random.fold_in(key_of[7], part), 8)
    q_latent = draw_q_latent(jax.random.fold_in(jax.random.fold_in(key_of[7], part), 71), part)
    q_rope = noise(own_keys[1], (H, NEW * ROPE), 1.0, 6.0)
    cache_latent = draw_cache_latent(jax.random.fold_in(jax.random.fold_in(key_of[7], part), 71), part)
    cache_rope = noise(own_keys[3], (NBLK, ROPE, BLK), 1.0, 6.0, ((0, 16),))
    new_latent = draw_new_latent(jax.random.fold_in(jax.random.fold_in(key_of[7], part), 71), part)
    new_rope = noise(own_keys[5], (NEW, ROPE), 1.0, 6.0)
    removed = draw_removed(jax.random.fold_in(jax.random.fold_in(key_of[7], part), 71), part)
    return dict(q_latent=q_latent, q_rope=q_rope, cache_latent=cache_latent, cache_rope=cache_rope, new_latent=new_latent, new_rope=new_rope, removed=removed)


floor_value = -1.0e30
score_scale = 192.0 ** -0.5


def rope_tables(rope_width):
    halves = rope_width // 2
    frequencies = 10000.0 ** (-2.0 * np.arange(halves) / rope_width)
    coarse = np.mod(4096.0 * frequencies, 2.0 * np.pi)
    middle = np.mod(64.0 * frequencies, 2.0 * np.pi)
    return jnp.asarray(frequencies, jnp.float32), jnp.asarray(coarse, jnp.float32), jnp.asarray(middle, jnp.float32)


def turn_angles(shift_rows, rope_width):
    frequencies, coarse, middle = rope_tables(rope_width)
    magnitude = jnp.abs(shift_rows)
    signed = jnp.where(shift_rows < 0, -1.0, 1.0).astype(jnp.float32)
    upper_part = (magnitude // 4096).astype(jnp.float32)[..., None]
    centre_part = ((magnitude // 64) % 64).astype(jnp.float32)[..., None]
    lowest_part = (magnitude % 64).astype(jnp.float32)[..., None]
    angles = upper_part * coarse + centre_part * middle + lowest_part * frequencies
    return jnp.cos(angles), signed[..., None] * jnp.sin(angles)


def rotate_last(values, cosine, sine_part):
    halves = values.shape[-1] // 2
    first_half = values[..., :halves]
    second_half = values[..., halves:]
    return jnp.concatenate([first_half * cosine - second_half * sine_part, first_half * sine_part + second_half * cosine], axis=-1)


def rotate_middle(values, cosine, sine_part):
    halves = values.shape[1] // 2
    first_half = values[:, :halves, :]
    second_half = values[:, halves:, :]
    return jnp.concatenate([first_half * cosine - second_half * sine_part, first_half * sine_part + second_half * cosine], axis=1)


def span_info(removed, total_blocks, block_rows):
    starts = removed[:, 0]
    finishes = removed[:, 1]
    block_ids = jnp.arange(total_blocks, dtype=jnp.int32)
    inside = (block_ids[:, None] >= starts[None, :]) & (block_ids[:, None] < finishes[None, :])
    kept_block = jnp.logical_not(jnp.any(inside, axis=1))
    drop_before = block_rows * jnp.sum(jnp.clip(block_ids[:, None], starts[None, :], finishes[None, :]) - starts[None, :], axis=1)
    kept_rows = total_blocks * block_rows - block_rows * jnp.sum(finishes - starts)
    return kept_block, drop_before.astype(jnp.int32), kept_rows.astype(jnp.int32)


def reference(q_latent, q_rope, cache_latent, cache_rope, new_latent, new_rope, removed):
    kept_block, drop_before, kept_rows = span_info(removed, NBLK, BLK)
    cosine, sine_part = turn_angles(-drop_before, ROPE)
    cache_keys = rotate_middle(cache_rope.astype(jnp.float32), cosine[:, :, None], sine_part[:, :, None]).astype(jnp.bfloat16)
    positions = kept_rows + jnp.arange(NEW, dtype=jnp.int32)
    query_cos, query_sin = turn_angles(positions, ROPE)
    queries_rope = rotate_last(q_rope.reshape(H, NEW, ROPE).astype(jnp.float32), query_cos, query_sin).astype(jnp.bfloat16)
    new_keys = rotate_last(new_rope.astype(jnp.float32), query_cos, query_sin).astype(jnp.bfloat16)
    latent_cols = cache_latent.reshape(CTX, LAT).T
    key_cols = jnp.transpose(cache_keys, (1, 0, 2)).reshape(ROPE, CTX)
    latent_blocks = cache_latent.astype(jnp.float32)
    causal = jnp.arange(NEW, dtype=jnp.int32)[None, :] <= jnp.arange(NEW, dtype=jnp.int32)[:, None]
    kept_flags = kept_block[None, :]

    def one_head(operands):
        head_latent, head_rope = operands
        scores = (jnp.dot(head_latent, latent_cols, preferred_element_type=jnp.float32) + jnp.dot(head_rope, key_cols, preferred_element_type=jnp.float32)) * score_scale
        scores = scores.reshape(NEW, NBLK, BLK)
        block_max = jnp.max(scores, axis=2)
        weights = jnp.exp(scores - block_max[:, :, None]).astype(jnp.bfloat16)
        block_sum = jnp.sum(weights.astype(jnp.float32), axis=2)
        block_out = jnp.einsum('tbr,brd->tbd', weights.astype(jnp.float32), latent_blocks)
        new_scores = (jnp.dot(head_latent, new_latent.T, preferred_element_type=jnp.float32) + jnp.dot(head_rope, new_keys.T, preferred_element_type=jnp.float32)) * score_scale
        masked = jnp.where(causal, new_scores, floor_value)
        new_max = jnp.max(masked, axis=1)
        new_weights = jnp.where(causal, jnp.exp(masked - new_max[:, None]), 0.0).astype(jnp.bfloat16)
        new_sum = jnp.sum(new_weights.astype(jnp.float32), axis=1)
        new_out = jnp.dot(new_weights, new_latent, preferred_element_type=jnp.float32)
        lifted = jnp.where(kept_flags, block_max, floor_value)
        top_score = jnp.maximum(jnp.max(lifted, axis=1), new_max)
        block_part = jnp.where(kept_flags, jnp.exp(lifted - top_score[:, None]), 0.0)
        new_part = jnp.exp(new_max - top_score)
        numerator = jnp.sum(block_out * block_part[:, :, None], axis=1) + new_out * new_part[:, None]
        denominator = jnp.sum(block_sum * block_part, axis=1) + new_sum * new_part
        return (numerator / denominator[:, None]).astype(jnp.bfloat16)

    return lax.map(one_head, (q_latent, queries_rope))
```

```python
import functools

import jax
import jax.numpy as jnp
import numpy as np
from jax import lax
from jax.experimental import pallas as pl
from jax.experimental.pallas import tpu as pltpu
from jax.sharding import PartitionSpec as P

floor_value = -1e30
score_scale = 192.0 ** (-0.5)
code_top = 32767.0
contract_last = (((1,), (1,)), ((), ()))


def rope_tables(rope_width):
    halves = rope_width // 2
    frequencies = 10000.0 ** (-2.0 * np.arange(halves) / rope_width)
    coarse = np.mod(4096.0 * frequencies, 2.0 * np.pi)
    middle = np.mod(64.0 * frequencies, 2.0 * np.pi)
    return (
        jnp.asarray(frequencies, jnp.float32),
        jnp.asarray(coarse, jnp.float32),
        jnp.asarray(middle, jnp.float32),
    )


def turn_angles(shift_rows, rope_width, axis):
    spread = (lambda v: v[:, None]) if axis == 0 else (lambda v: v[None, :])
    across = (lambda v: v[None, :]) if axis == 0 else (lambda v: v[:, None])
    frequencies, coarse, middle = (spread(t) for t in rope_tables(rope_width))
    magnitude = jnp.abs(shift_rows)
    signed = across(jnp.where(shift_rows < 0, -1.0, 1.0).astype(jnp.float32))
    upper_part = across((magnitude // 4096).astype(jnp.float32))
    centre_part = across((magnitude // 64 % 64).astype(jnp.float32))
    lowest_part = across((magnitude % 64).astype(jnp.float32))
    angles = upper_part * coarse + centre_part * middle + lowest_part * frequencies
    return (jnp.cos(angles), signed * jnp.sin(angles))


def rotate_last(values, cosine, sine_part):
    halves = values.shape[-1] // 2
    first_half = values[..., :halves]
    second_half = values[..., halves:]
    return jnp.concatenate(
        [
            first_half * cosine - second_half * sine_part,
            first_half * sine_part + second_half * cosine,
        ],
        axis=-1,
    )


def rotate_keys(rope_ref, cos_ref, sin_ref, keys_ref, first):
    count, width, _ = rope_ref.shape
    halves = width // 2
    for b in range(count):
        cosine = cos_ref[:, first + b : first + b + 1]
        sine_part = sin_ref[:, first + b : first + b + 1]
        upper = rope_ref[b, :halves, :].astype(jnp.float32)
        lower = rope_ref[b, halves:, :].astype(jnp.float32)
        keys_ref[first + b, :halves, :] = (upper * cosine - lower * sine_part).astype(jnp.bfloat16)
        keys_ref[first + b, halves:, :] = (upper * sine_part + lower * cosine).astype(jnp.bfloat16)


def absorb_block(query, rope, latent, keys, max_ref, sum_ref, acc_ref):
    scores = (
        lax.dot_general(query, latent, contract_last, preferred_element_type=jnp.float32)
        + jnp.dot(rope, keys, preferred_element_type=jnp.float32)
    ) * score_scale
    block_max = jnp.max(scores, axis=1, keepdims=True)
    weights = jnp.exp(scores - block_max).astype(jnp.bfloat16)
    block_sum = jnp.sum(weights.astype(jnp.float32), axis=1, keepdims=True)
    block_out = jnp.dot(weights, latent, preferred_element_type=jnp.float32)
    run_max = max_ref[...]
    new_max = jnp.maximum(run_max, block_max)
    old_scale = jnp.exp(run_max - new_max)
    add_scale = jnp.exp(block_max - new_max)
    max_ref[...] = new_max
    sum_ref[...] = sum_ref[...] * old_scale + block_sum * add_scale
    acc_ref[...] = acc_ref[...] * old_scale + block_out * add_scale


def attend(pieces, dest, kept, q_ref, r_ref, cos_ref, sin_ref, lat_refs, rope_refs, keys_ref, max_ref, sum_ref, acc_ref):
    step = pl.program_id(0)
    blocks = lat_refs[0].shape[0]

    @pl.when(step == 0)
    def _():
        for p in range(pieces):
            rotate_keys(rope_refs[p], cos_ref, sin_ref, keys_ref, p * blocks)

    for p in range(pieces):
        for b in range(blocks):

            @pl.when(kept[p * blocks + b] != 0)
            def _(p=p, b=b):
                absorb_block(
                    q_ref[0], r_ref[0], lat_refs[p][b], keys_ref[p * blocks + b], max_ref, sum_ref, acc_ref
                )


def first_kernel(pieces, dest, kept, q_ref, r_ref, cos_ref, sin_ref, *rest):
    lat_refs, rope_refs = rest[:pieces], rest[pieces : 2 * pieces]
    stat_ref, acc_out, keys_ref, max_ref, sum_ref, acc_ref = rest[2 * pieces :]
    max_ref[...] = jnp.full_like(max_ref, floor_value)
    sum_ref[...] = jnp.zeros_like(sum_ref)
    acc_ref[...] = jnp.zeros_like(acc_ref)
    attend(pieces, dest, kept, q_ref, r_ref, cos_ref, sin_ref, lat_refs, rope_refs, keys_ref, max_ref, sum_ref, acc_ref)
    lane = lax.broadcasted_iota(jnp.int32, stat_ref.shape[1:], 1)
    stat_ref[0] = jnp.where(lane == 0, max_ref[...], sum_ref[...])
    acc_out[0] = acc_ref[...]


def second_kernel(pieces, groups, dest, kept, q_ref, r_ref, cos_ref, sin_ref, stat_in, acc_in, *rest):
    lat_refs, rope_refs = rest[:pieces], rest[pieces : 2 * pieces]
    rest = rest[2 * pieces :]
    code_refs, stat_refs = rest[:groups], rest[groups : 2 * groups]
    keys_ref, max_ref, sum_ref, acc_ref = rest[2 * groups :]
    max_ref[...] = stat_in[0, :, 0:1]
    sum_ref[...] = stat_in[0, :, 1:2]
    acc_ref[...] = acc_in[0]
    attend(pieces, dest, kept, q_ref, r_ref, cos_ref, sin_ref, lat_refs, rope_refs, keys_ref, max_ref, sum_ref, acc_ref)
    acc = acc_ref[...]
    rows = acc.shape[0]
    reach = jnp.maximum(jnp.max(jnp.abs(acc), axis=1, keepdims=True), 1e-30)
    codes = jnp.round(acc * (code_top / reach)).astype(jnp.int32).astype(jnp.int16)
    lane = lax.broadcasted_iota(jnp.int32, (rows, 128), 1)
    stats = jnp.where(lane == 0, max_ref[...], jnp.where(lane == 1, sum_ref[...], reach * (1.0 / code_top)))
    stats = stats.T[0:8, :]
    step = pl.program_id(0)
    for k in range(groups):

        @pl.when(step == k)
        def _(k=k):
            code_refs[k][...] = codes
            stat_refs[k][...] = stats


def new_kernel(index, q_ref, r_ref, lat_ref, keys_ref, stat_ref, out_ref, *, tokens):
    query, rope = q_ref[0], r_ref[0]
    rows = query.shape[0]
    latent = lat_ref[...]
    scores = (
        lax.dot_general(query, latent, contract_last, preferred_element_type=jnp.float32)
        + lax.dot_general(rope, keys_ref[...], contract_last, preferred_element_type=jnp.float32)
    ) * score_scale
    row_token = lax.broadcasted_iota(jnp.int32, scores.shape, 0) % tokens
    causal = lax.broadcasted_iota(jnp.int32, scores.shape, 1) <= row_token
    masked = jnp.where(causal, scores, floor_value)
    new_max = jnp.max(masked, axis=1, keepdims=True)
    weights = jnp.where(causal, jnp.exp(masked - new_max), 0.0).astype(jnp.bfloat16)
    new_sum = jnp.sum(weights.astype(jnp.float32), axis=1, keepdims=True)
    out_ref[...] = jnp.dot(weights, latent, preferred_element_type=jnp.float32)
    lane = lax.broadcasted_iota(jnp.int32, (rows, 128), 1)
    stat_ref[...] = jnp.where(lane == 0, new_max, new_sum)


def final_kernel(groups, stat_new, out_new, *rest):
    code_refs, stat_refs = rest[:groups], rest[groups : 2 * groups]
    result = rest[2 * groups]
    rows = out_new.shape[0]
    maxima, sums, scales = [stat_new[:, 0:1]], [stat_new[:, 1:2]], [None]
    for k in range(groups):
        stats = jnp.concatenate([stat_refs[k][...], jnp.zeros((120, rows), jnp.float32)], axis=0).T
        maxima.append(stats[:, 0:1])
        sums.append(stats[:, 1:2])
        scales.append(stats[:, 2:3])
    top = functools.reduce(jnp.maximum, maxima)
    factors = [jnp.exp(m - top) for m in maxima]
    total = functools.reduce(jnp.add, [f * s for f, s in zip(factors, sums)])
    numerator = out_new[...] * factors[0]
    for k in range(groups):
        part = code_refs[k][...].astype(jnp.int32).astype(jnp.float32)
        numerator = numerator + part * (scales[k + 1] * factors[k + 1])
    result[...] = (numerator / total).astype(jnp.bfloat16)


def whole(shape):
    return pl.BlockSpec(shape, lambda *_: (0,) * len(shape))


def gather_size(devices):
    size = 1
    while (2 * size) ** 2 <= devices and devices % (2 * size) == 0:
        size *= 2
    return size


def shards(q_latent, q_rope, cache_latent, cache_rope, new_latent, new_rope, removed):
    devices = lax.axis_size("ctx")
    me = lax.axis_index("ctx")
    blocks, block_rows, lat_width = cache_latent.shape
    head_count, tokens = (q_latent.shape[0], q_latent.shape[1])
    rope_width = new_rope.shape[1]
    own_heads = head_count // devices
    rows = own_heads * tokens
    size = gather_size(devices)
    groups = devices // size

    def swap(value, k):
        return lax.ppermute(value, "ctx", [(i, i ^ k) for i in range(devices)])

    latents, ropes = {0: cache_latent}, {0: cache_rope}
    for k in range(2, size, 2):
        latents[k], ropes[k] = swap(cache_latent, k), swap(cache_rope, k)
    if size > 1:
        latents[1], ropes[1] = swap(cache_latent, 1), swap(cache_rope, 1)
    for k in range(2, size, 2):
        latents[k + 1], ropes[k + 1] = swap(latents[k], 1), swap(ropes[k], 1)

    starts, finishes = removed[:, 0][:, None], removed[:, 1][:, None]
    members = me ^ jnp.arange(size, dtype=jnp.int32)
    block_ids = (members[:, None] * blocks + jnp.arange(blocks, dtype=jnp.int32)[None, :]).reshape(1, -1)
    inside = (block_ids >= starts) & (block_ids < finishes)
    kept = jnp.logical_not(jnp.any(inside, axis=0)).astype(jnp.int32)
    drop = block_rows * jnp.sum(jnp.clip(block_ids, starts, finishes) - starts, axis=0)
    kept_rows = blocks * devices * block_rows - block_rows * jnp.sum(finishes - starts)
    cosine, sine_part = turn_angles(-drop, rope_width, 0)
    positions = kept_rows + jnp.arange(tokens, dtype=jnp.int32)
    query_cos, query_sin = turn_angles(positions, rope_width, 1)
    new_keys = rotate_last(new_rope.astype(jnp.float32), query_cos, query_sin).astype(jnp.bfloat16)

    dest = me ^ (size * jnp.arange(groups, dtype=jnp.int32))
    slabs = q_latent.reshape(devices, rows, lat_width)
    rope_slabs = jnp.take(q_rope.reshape(devices, own_heads, tokens * rope_width), dest, axis=0)
    rope_slabs = rotate_last(
        rope_slabs.reshape(groups, own_heads, tokens, rope_width).astype(jnp.float32), query_cos, query_sin
    ).astype(jnp.bfloat16).reshape(groups, rows, rope_width)

    def run(kernel, members, extra_in, extra_specs, out_shape, out_specs):
        count = len(members)
        span = slice(members[0] * blocks, (members[-1] + 1) * blocks)
        lat_in = [latents[k] for k in members]
        rope_in = [ropes[k] for k in members]
        tables = [cosine[:, span], sine_part[:, span]]
        flops = 2 * groups * rows * count * blocks * block_rows * (2 * lat_width + rope_width)
        return pl.pallas_call(
            functools.partial(kernel, count),
            grid_spec=pltpu.PrefetchScalarGridSpec(
                num_scalar_prefetch=2,
                grid=(groups,),
                in_specs=[
                    pl.BlockSpec((1, rows, lat_width), lambda t, d, _: (d[t], 0, 0)),
                    pl.BlockSpec((1, rows, rope_width), lambda t, *_: (t, 0, 0)),
                    *[whole(t.shape) for t in tables],
                    *extra_specs,
                    *[whole(v.shape) for v in lat_in],
                    *[whole(v.shape) for v in rope_in],
                ],
                out_specs=out_specs,
                scratch_shapes=[
                    pltpu.VMEM((count * blocks, rope_width, block_rows), jnp.bfloat16),
                    pltpu.VMEM((rows, 1), jnp.float32),
                    pltpu.VMEM((rows, 1), jnp.float32),
                    pltpu.VMEM((rows, lat_width), jnp.float32),
                ],
            ),
            out_shape=out_shape,
            cost_estimate=pl.CostEstimate(
                flops=flops, bytes_accessed=4 * groups * rows * lat_width, transcendentals=0
            ),
        )(dest, kept[span], slabs, rope_slabs, *tables, *extra_in, *lat_in, *rope_in)

    per_step = lambda *shape: pl.BlockSpec((1, *shape), lambda t, *_: (t, 0, 0))
    near = list(range(min(2, size)))
    far = list(range(len(near), size))
    stat, acc = run(
        first_kernel,
        near,
        [],
        [],
        [
            jax.ShapeDtypeStruct((groups, rows, 128), jnp.float32),
            jax.ShapeDtypeStruct((groups, rows, lat_width), jnp.float32),
        ],
        [per_step(rows, 128), per_step(rows, lat_width)],
    )
    new_stat, new_out = pl.pallas_call(
        functools.partial(new_kernel, tokens=tokens),
        grid_spec=pltpu.PrefetchScalarGridSpec(
            num_scalar_prefetch=1,
            grid=(1,),
            in_specs=[
                pl.BlockSpec((1, rows, lat_width), lambda t, d: (d[0], 0, 0)),
                pl.BlockSpec((1, rows, rope_width), lambda t, d: (0, 0, 0)),
                whole(new_latent.shape),
                whole(new_keys.shape),
            ],
            out_specs=[whole((rows, 128)), whole((rows, lat_width))],
        ),
        out_shape=[
            jax.ShapeDtypeStruct((rows, 128), jnp.float32),
            jax.ShapeDtypeStruct((rows, lat_width), jnp.float32),
        ],
        cost_estimate=pl.CostEstimate(flops=10**8, bytes_accessed=10**6, transcendentals=0),
    )(dest, slabs, rope_slabs, new_latent, new_keys)
    sent = run(
        lambda count, *refs: second_kernel(count, groups, *refs),
        far,
        [stat, acc],
        [per_step(rows, 128), per_step(rows, lat_width)],
        [jax.ShapeDtypeStruct((rows, lat_width), jnp.int16)] * groups
        + [jax.ShapeDtypeStruct((8, rows), jnp.float32)] * groups,
        [whole((rows, lat_width))] * groups + [whole((8, rows))] * groups,
    )
    codes, stats = list(sent[:groups]), list(sent[groups:])
    for k in range(1, groups):
        codes[k] = swap(codes[k], k * size)
        stats[k] = swap(stats[k], k * size)
    attended = pl.pallas_call(
        functools.partial(final_kernel, groups),
        out_shape=jax.ShapeDtypeStruct((rows, lat_width), jnp.bfloat16),
        cost_estimate=pl.CostEstimate(flops=10**6, bytes_accessed=10**6, transcendentals=0),
    )(new_stat, new_out, *codes, *stats)
    return attended.reshape(own_heads, tokens, lat_width)


def solution(mesh):
    in_specs = (
        P(None, "req", None),
        P(None, "req"),
        P(("req", "ctx"), None, None),
        P(("req", "ctx"), None, None),
        P("req", None),
        P("req", None),
        P("req", None),
    )
    out_specs = P("ctx", "req", None)
    return jax.shard_map(shards, mesh=mesh, in_specs=in_specs, out_specs=out_specs, check_vma=False)
```

```python
import functools

import jax
import jax.numpy as jnp
import numpy as np
from jax import lax
from jax.experimental import pallas as pl
from jax.experimental.pallas import tpu as pltpu
from jax.sharding import PartitionSpec as P

floor_value = -1e30
score_scale = 192.0 ** (-0.5)
code_top = 32767.0
contract_last = (((1,), (1,)), ((), ()))
contract_first = (((0,), (0,)), ((), ()))


def rope_tables(rope_width):
    halves = rope_width // 2
    frequencies = 10000.0 ** (-2.0 * np.arange(halves) / rope_width)
    coarse = np.mod(4096.0 * frequencies, 2.0 * np.pi)
    middle = np.mod(64.0 * frequencies, 2.0 * np.pi)
    return (
        jnp.asarray(frequencies, jnp.float32),
        jnp.asarray(coarse, jnp.float32),
        jnp.asarray(middle, jnp.float32),
    )


def turn_angles(shift_rows, rope_width, axis):
    spread = (lambda v: v[:, None]) if axis == 0 else (lambda v: v[None, :])
    across = (lambda v: v[None, :]) if axis == 0 else (lambda v: v[:, None])
    frequencies, coarse, middle = (spread(t) for t in rope_tables(rope_width))
    magnitude = jnp.abs(shift_rows)
    signed = across(jnp.where(shift_rows < 0, -1.0, 1.0).astype(jnp.float32))
    upper_part = across((magnitude // 4096).astype(jnp.float32))
    centre_part = across((magnitude // 64 % 64).astype(jnp.float32))
    lowest_part = across((magnitude % 64).astype(jnp.float32))
    angles = upper_part * coarse + centre_part * middle + lowest_part * frequencies
    return (jnp.cos(angles), signed * jnp.sin(angles))


def rotate_last(values, cosine, sine_part):
    halves = values.shape[-1] // 2
    first_half = values[..., :halves]
    second_half = values[..., halves:]
    return jnp.concatenate(
        [
            first_half * cosine - second_half * sine_part,
            first_half * sine_part + second_half * cosine,
        ],
        axis=-1,
    )


def fill_blocks(lat_refs, rope_refs, cos_ref, sin_ref, turned_ref, keys_ref):
    position = 0
    for lat_ref, rope_ref in zip(lat_refs, rope_refs):
        count, width, _ = rope_ref.shape
        halves = width // 2
        for b in range(count):
            cosine = cos_ref[:, position : position + 1]
            sine_part = sin_ref[:, position : position + 1]
            upper = rope_ref[b, :halves, :].astype(jnp.float32)
            lower = rope_ref[b, halves:, :].astype(jnp.float32)
            keys = jnp.concatenate(
                [upper * cosine - lower * sine_part, upper * sine_part + lower * cosine], axis=0
            )
            keys_ref[position] = keys.T.astype(jnp.bfloat16)
            turned_ref[position] = lat_ref[b].T
            position += 1


def stack(refs, ids):
    parts = [refs[i][0] for i in ids]
    return parts[0] if len(parts) == 1 else jnp.concatenate(parts, axis=0)


def absorb(query, rope, kept, lat_refs, turned_ref, keys_ref, run_max, run_sum, old_acc):
    blocks = [ref[b] for ref in lat_refs for b in range(ref.shape[0])]
    lifted, flags, sums, weights = [], [], [], []
    for b, latent in enumerate(blocks):
        scores = (
            lax.dot_general(latent, query, contract_last, preferred_element_type=jnp.float32)
            + lax.dot_general(keys_ref[b], rope, contract_last, preferred_element_type=jnp.float32)
        ) * score_scale
        block_max = jnp.max(scores, axis=0, keepdims=True)
        weight = jnp.exp(scores - block_max).astype(jnp.bfloat16)
        sums.append(jnp.sum(weight.astype(jnp.float32), axis=0, keepdims=True))
        weights.append(weight)
        flags.append(kept[b] != 0)
        lifted.append(jnp.where(flags[-1], block_max, floor_value))
    new_max = functools.reduce(jnp.maximum, lifted, run_max)
    old_scale = jnp.exp(run_max - new_max)
    factors = [jnp.where(f, jnp.exp(m - new_max), 0.0) for f, m in zip(flags, lifted)]
    new_sum = run_sum * old_scale
    for s, f in zip(sums, factors):
        new_sum = new_sum + s * f
    width = turned_ref.shape[1]
    chunk = min(128, width)
    acc = []
    for c in range(0, width, chunk):
        total = None if old_acc is None else old_acc(c, chunk) * old_scale
        for b, weight in enumerate(weights):
            term = jnp.dot(turned_ref[b, c : c + chunk, :], weight, preferred_element_type=jnp.float32) * factors[b]
            total = term if total is None else total + term
        acc.append(total)
    return new_max, new_sum, acc


def pack_stats(*rows):
    lanes = rows[0].shape[1]
    return jnp.concatenate([*rows, jnp.zeros((8 - len(rows), lanes), jnp.float32)], axis=0)


def encode(acc):
    reach = functools.reduce(jnp.maximum, [jnp.max(jnp.abs(a), axis=0, keepdims=True) for a in acc])
    reach = jnp.maximum(reach, 1e-30)
    gain = code_top / reach
    codes = [jnp.round(a * gain).astype(jnp.int32).astype(jnp.int16) for a in acc]
    return codes, reach * (1.0 / code_top)


def decode(codes):
    return codes.astype(jnp.int32).astype(jnp.float32)


def write_coded(acc, new_max, new_sum, code_refs, stat_refs, ids, lanes):
    codes, scale = encode(acc)
    stats = pack_stats(new_max, new_sum, scale)
    chunk = codes[0].shape[0]
    for n, i in enumerate(ids):
        span = slice(n * lanes, (n + 1) * lanes)
        stat_refs[i][...] = stats[:, span]
        for c, part in enumerate(codes):
            code_refs[i][c * chunk : (c + 1) * chunk, :] = part[:, span]


def tiles_of(count, lanes, most=256):
    step = max(1, most // lanes)
    return [list(range(i, min(i + step, count))) for i in range(0, count, step)]


def queries(refs, rope_ref, ids, lanes):
    span = slice(ids[0] * lanes, (ids[-1] + 1) * lanes)
    query = stack(refs, ids) if len(refs) > 1 else refs[0][0, span, :]
    return query, rope_ref[span, :]


def early_kernel(plan, dest, kept, *refs):
    slots, lanes, parts, per, n_q = plan
    q_refs, refs = refs[:n_q], refs[n_q:]
    rope_ref, cos_ref, sin_ref, refs = *refs[:3], refs[3:]
    lat_refs, rope_refs, refs = refs[:parts], refs[parts : 2 * parts], refs[2 * parts :]
    sends = slots // per
    code_refs, stat_refs = refs[:sends], refs[sends : 2 * sends]
    turned_ref, keys_ref = refs[2 * sends :]
    fill_blocks(lat_refs, rope_refs, cos_ref, sin_ref, turned_ref, keys_ref)
    for ids in tiles_of(slots, lanes):
        query, rope = queries(q_refs, rope_ref, ids, lanes)
        run_max = jnp.full((1, query.shape[0]), floor_value, jnp.float32)
        new_max, new_sum, acc = absorb(
            query, rope, kept, lat_refs, turned_ref, keys_ref, run_max, jnp.zeros_like(run_max), None
        )
        write_coded(
            acc, new_max, new_sum, code_refs, stat_refs, range(ids[0] // per, (ids[-1] + 1) // per), lanes * per
        )


def near_kernel(plan, dest, kept, *refs):
    slots, lanes, parts, tokens, n_q = plan
    q_refs, refs = refs[:n_q], refs[n_q:]
    rope_ref, cos_ref, sin_ref, own_q, own_rope, new_lat, new_keys, refs = *refs[:7], refs[7:]
    lat_refs, rope_refs, refs = refs[:parts], refs[parts : 2 * parts], refs[2 * parts :]
    stat_out, acc_out, new_stat, new_out, turned_ref, keys_ref = refs
    fill_blocks(lat_refs, rope_refs, cos_ref, sin_ref, turned_ref, keys_ref)
    for ids in tiles_of(slots, lanes):
        query, rope = queries(q_refs, rope_ref, ids, lanes)
        span = slice(ids[0] * lanes, (ids[-1] + 1) * lanes)
        run_max = jnp.full((1, query.shape[0]), floor_value, jnp.float32)
        new_max, new_sum, acc = absorb(
            query, rope, kept, lat_refs, turned_ref, keys_ref, run_max, jnp.zeros_like(run_max), None
        )
        stat_out[:, span] = pack_stats(new_max, new_sum)
        chunk = acc[0].shape[0]
        for c, part in enumerate(acc):
            acc_out[c * chunk : (c + 1) * chunk, span] = part
    latent = new_lat[...]
    scores = (
        lax.dot_general(latent, own_q[0], contract_last, preferred_element_type=jnp.float32)
        + lax.dot_general(new_keys[...], own_rope[...], contract_last, preferred_element_type=jnp.float32)
    ) * score_scale
    row_token = lax.broadcasted_iota(jnp.int32, scores.shape, 1) % tokens
    causal = lax.broadcasted_iota(jnp.int32, scores.shape, 0) <= row_token
    masked = jnp.where(causal, scores, floor_value)
    top = jnp.max(masked, axis=0, keepdims=True)
    weights = jnp.where(causal, jnp.exp(masked - top), 0.0).astype(jnp.bfloat16)
    new_stat[...] = pack_stats(top, jnp.sum(weights.astype(jnp.float32), axis=0, keepdims=True))
    new_out[...] = lax.dot_general(latent, weights, contract_first, preferred_element_type=jnp.float32)


def far_kernel(plan, dest, kept, *refs):
    slots, lanes, parts, n_q = plan
    q_refs, refs = refs[:n_q], refs[n_q:]
    rope_ref, cos_ref, sin_ref, stat_in, acc_in, refs = *refs[:5], refs[5:]
    lat_refs, rope_refs, refs = refs[:parts], refs[parts : 2 * parts], refs[2 * parts :]
    code_refs, stat_refs = refs[:slots], refs[slots : 2 * slots]
    turned_ref, keys_ref = refs[2 * slots :]
    fill_blocks(lat_refs, rope_refs, cos_ref, sin_ref, turned_ref, keys_ref)
    for ids in tiles_of(slots, lanes):
        query, rope = queries(q_refs, rope_ref, ids, lanes)
        span = slice(ids[0] * lanes, (ids[-1] + 1) * lanes)
        new_max, new_sum, acc = absorb(
            query,
            rope,
            kept,
            lat_refs,
            turned_ref,
            keys_ref,
            stat_in[0:1, span],
            stat_in[1:2, span],
            lambda c, size, span=span: acc_in[c : c + size, span],
        )
        write_coded(acc, new_max, new_sum, code_refs, stat_refs, ids, lanes)


def join(stats, values, first=None):
    top = functools.reduce(jnp.maximum, [s[0] for s in stats])
    factors = [jnp.exp(s[0] - top) for s in stats]
    total = functools.reduce(jnp.add, [f * s[1] for f, s in zip(factors, stats)])
    return top, factors, total


def middle_kernel(plan, *refs):
    lanes, per, count = plan
    code_refs, stat_refs, refs = refs[:count], refs[count : 2 * count], refs[2 * count :]
    own_out, own_stat, refs = refs[0], refs[1], refs[2:]
    sent, sent_stats = refs[: per - 1], refs[per - 1 :]
    stats = [r[...] for r in stat_refs]
    top, factors, total = join([(s[0:1], s[1:2]) for s in stats], None)
    gains = [f * s[2:3] for f, s in zip(factors, stats)]
    width = own_out.shape[0]
    chunk = min(128, width)
    acc = []
    for c in range(0, width, chunk):
        terms = [decode(r[c : c + chunk, :]) * g for r, g in zip(code_refs, gains)]
        acc.append(functools.reduce(jnp.add, terms))
    for c, part in enumerate(acc):
        own_out[c * chunk : (c + 1) * chunk, :] = part[:, :lanes]
    own_stat[...] = pack_stats(top, total)[:, :lanes]
    codes, scale = encode(acc)
    stats = pack_stats(top, total, scale)
    for n in range(per - 1):
        span = slice((n + 1) * lanes, (n + 2) * lanes)
        sent_stats[n][...] = stats[:, span]
        for c, part in enumerate(codes):
            sent[n][c * chunk : (c + 1) * chunk, :] = part[:, span]


def last_kernel(plan, *refs):
    lanes_a, lanes_b, groups, per = plan
    new_stat, new_out, refs = refs[0], refs[1], refs[2:]
    codes_a, stats_a, refs = refs[:groups], refs[groups : 2 * groups], refs[2 * groups :]
    result = refs[-1]
    sections = [(slice(0, lanes_a), [], codes_a, stats_a)]
    if lanes_b:
        own_b, own_stat, refs = refs[0], refs[1], refs[2:]
        sections.append((slice(lanes_a, lanes_a + lanes_b), [(own_b, own_stat)], refs[: per - 1], refs[per - 1 : -1]))
    width = new_out.shape[0]
    chunk = min(128, width)
    prepared = []
    for span, plain, codes, coded_stats in sections:
        stats = [new_stat[:, span]] + [s[...] for _, s in plain] + [s[...] for s in coded_stats]
        _, factors, total = join([(s[0:1], s[1:2]) for s in stats], None)
        known = 1 + len(plain)
        gains = factors[:known] + [f * s[2:3] for f, s in zip(factors[known:], stats[known:])]
        prepared.append((gains, total))
    for c in range(0, width, chunk):
        piece = slice(c, c + chunk)
        columns = []
        for (span, plain, codes, _), (gains, total) in zip(sections, prepared):
            values = [new_out[piece, span]] + [v[piece, :] for v, _ in plain] + [decode(v[piece, :]) for v in codes]
            numerator = functools.reduce(jnp.add, [v * g for v, g in zip(values, gains)])
            columns.append(numerator / total)
        merged = columns[0] if len(columns) == 1 else jnp.concatenate(columns, axis=1)
        result[:, piece] = merged.T.astype(jnp.bfloat16)


def whole(shape):
    return pl.BlockSpec(tuple(shape), lambda *_: (0,) * len(shape))


def gather_size(devices):
    size = 1
    while (2 * size) ** 2 <= devices and devices % (2 * size) == 0:
        size *= 2
    return size


def shards(q_latent, q_rope, cache_latent, cache_rope, new_latent, new_rope, removed):
    devices = lax.axis_size("ctx")
    me = lax.axis_index("ctx")
    blocks, block_rows, lat_width = cache_latent.shape
    head_count, tokens = (q_latent.shape[0], q_latent.shape[1])
    rope_width = new_rope.shape[1]
    own_heads = head_count // devices
    rows = own_heads * tokens
    size = gather_size(devices)
    pair = min(2, size)
    per = size // pair
    groups = devices // size
    lanes_b = rows // 3 if rows % 192 == 0 and per > 1 else 0
    lanes_a = rows - lanes_b

    def swap(value, k):
        return lax.ppermute(value, "ctx", [(i, i ^ k) for i in range(devices)])

    latents, ropes = {0: cache_latent}, {0: cache_rope}
    if size > 1:
        latents[1], ropes[1] = swap(cache_latent, 1), swap(cache_rope, 1)
    for k in range(2, size, 2):
        latents[k], ropes[k] = swap(cache_latent, k), swap(cache_rope, k)
    for k in range(2, size, 2):
        latents[k + 1], ropes[k + 1] = swap(latents[k], 1), swap(ropes[k], 1)

    starts, finishes = removed[:, 0][:, None], removed[:, 1][:, None]
    members = me ^ jnp.arange(size, dtype=jnp.int32)
    block_ids = (members[:, None] * blocks + jnp.arange(blocks, dtype=jnp.int32)[None, :]).reshape(1, -1)
    inside = (block_ids >= starts) & (block_ids < finishes)
    kept = jnp.logical_not(jnp.any(inside, axis=0)).astype(jnp.int32)
    drop = block_rows * jnp.sum(jnp.clip(block_ids, starts, finishes) - starts, axis=0)
    kept_rows = blocks * devices * block_rows - block_rows * jnp.sum(finishes - starts)
    cosine, sine_part = turn_angles(-drop, rope_width, 0)
    positions = kept_rows + jnp.arange(tokens, dtype=jnp.int32)
    query_cos, query_sin = turn_angles(positions, rope_width, 1)
    new_keys = rotate_last(new_rope.astype(jnp.float32), query_cos, query_sin).astype(jnp.bfloat16)

    along_z = size * jnp.arange(groups, dtype=jnp.int32)
    along_x = pair * jnp.arange(per, dtype=jnp.int32)
    dest = (me ^ along_z[:, None] ^ along_x[None, :]).reshape(-1)
    dest_a = me ^ along_z
    slabs = q_latent.reshape(devices, rows, lat_width)
    packed = q_rope.reshape(devices, own_heads, tokens * rope_width)
    turn = dest if lanes_b else dest_a
    rope_slabs = jnp.take(packed, turn, axis=0).reshape(turn.shape[0], own_heads, tokens, rope_width)
    rope_slabs = rotate_last(rope_slabs.astype(jnp.float32), query_cos, query_sin)
    rope_slabs = rope_slabs.astype(jnp.bfloat16).reshape(groups, -1, rows, rope_width)
    rope_a = rope_slabs[:, 0, :lanes_a].reshape(groups * lanes_a, rope_width)
    own_rope = rope_slabs[0, 0]

    def call(kernel, scalars, ins, specs, outs, scratch=(), flops=10**7):
        return pl.pallas_call(
            kernel,
            grid_spec=pltpu.PrefetchScalarGridSpec(
                num_scalar_prefetch=len(scalars),
                grid=(1,),
                in_specs=specs,
                out_specs=[whole(o.shape) for o in outs],
                scratch_shapes=list(scratch),
            ),
            out_shape=outs,
            cost_estimate=pl.CostEstimate(flops=flops, bytes_accessed=10**6, transcendentals=0),
        )(*scalars, *ins)

    def query_rows(ids, count, first):
        number = ids.shape[0]
        if count % 16 == 0 and first % count == 0:
            at = first // count
            return [slabs] * number, [
                pl.BlockSpec((1, count, lat_width), lambda t, d, *_, i=i: (d[i], at, 0)) for i in range(number)
            ]
        chosen = jnp.take(slabs, ids, axis=0)[:, first : first + count].reshape(1, number * count, lat_width)
        return [chosen], [whole(chosen.shape)]

    def cache_of(members):
        span = slice(members[0] * blocks, (members[-1] + 1) * blocks)
        arrays = [latents[k] for k in members] + [ropes[k] for k in members]
        scratch = [
            pltpu.VMEM((len(members) * blocks, lat_width, block_rows), jnp.bfloat16),
            pltpu.VMEM((len(members) * blocks, block_rows, rope_width), jnp.bfloat16),
        ]
        return span, [cosine[:, span], sine_part[:, span]], arrays, scratch

    def shape(dtype, *dims):
        return jax.ShapeDtypeStruct(dims, dtype)

    near, far = list(range(pair)), list(range(pair, size))
    span, tables, arrays, scratch = cache_of(near)
    extras = [*tables]
    if lanes_b:
        rope_b = rope_slabs[:, :, lanes_a:].reshape(groups * per * lanes_b, rope_width)
        q_in, q_specs = query_rows(dest, lanes_b, lanes_a)
        ins = [rope_b, *tables, *arrays]
        out = call(
            functools.partial(early_kernel, (groups * per, lanes_b, pair, per, len(q_in))),
            [dest, kept[span]],
            [*q_in, *ins],
            [*q_specs, *[whole(v.shape) for v in ins]],
            [shape(jnp.int16, lat_width, per * lanes_b)] * groups + [shape(jnp.float32, 8, per * lanes_b)] * groups,
            scratch,
            10**9,
        )
        codes_b, stats_b = list(out[:groups]), list(out[groups:])
        for k in range(1, groups):
            codes_b[k], stats_b[k] = swap(codes_b[k], k * size), swap(stats_b[k], k * size)
    qa_in, qa_specs = query_rows(dest_a, lanes_a, 0)
    ins = [rope_a, *tables, slabs, own_rope, new_latent, new_keys, *arrays]
    specs = [whole(v.shape) for v in ins]
    specs[3] = pl.BlockSpec((1, rows, lat_width), lambda t, d, *_: (d[0], 0, 0))
    near_stat, near_acc, new_stat, new_out = call(
        functools.partial(near_kernel, (groups, lanes_a, pair, tokens, len(qa_in))),
        [dest_a, kept[span]],
        [*qa_in, *ins],
        [*qa_specs, *specs],
        [
            shape(jnp.float32, 8, groups * lanes_a),
            shape(jnp.float32, lat_width, groups * lanes_a),
            shape(jnp.float32, 8, rows),
            shape(jnp.float32, lat_width, rows),
        ],
        scratch,
        10**9,
    )
    span, tables, arrays, scratch = cache_of(far)
    ins = [rope_a, *tables, near_stat, near_acc, *arrays]
    out = call(
        functools.partial(far_kernel, (groups, lanes_a, len(far), len(qa_in))),
        [dest_a, kept[span]],
        [*qa_in, *ins],
        [*qa_specs, *[whole(v.shape) for v in ins]],
        [shape(jnp.int16, lat_width, lanes_a)] * groups + [shape(jnp.float32, 8, lanes_a)] * groups,
        scratch,
        10**9,
    )
    codes_a, stats_a = list(out[:groups]), list(out[groups:])
    for k in range(1, groups):
        codes_a[k], stats_a[k] = swap(codes_a[k], k * size), swap(stats_a[k], k * size)
    ins = [new_stat, new_out, *codes_a, *stats_a]
    if lanes_b:
        given = [*codes_b, *stats_b]
        out = call(
            functools.partial(middle_kernel, (lanes_b, per, groups)),
            [],
            given,
            [whole(v.shape) for v in given],
            [shape(jnp.float32, lat_width, lanes_b), shape(jnp.float32, 8, lanes_b)]
            + [shape(jnp.int16, lat_width, lanes_b)] * (per - 1)
            + [shape(jnp.float32, 8, lanes_b)] * (per - 1),
        )
        own_b, own_stat, sent, sent_stats = out[0], out[1], list(out[2 : 1 + per]), list(out[1 + per :])
        for n in range(per - 1):
            sent[n], sent_stats[n] = swap(sent[n], (n + 1) * pair), swap(sent_stats[n], (n + 1) * pair)
        ins = [*ins, own_b, own_stat, *sent, *sent_stats]
    (attended,) = call(
        functools.partial(last_kernel, (lanes_a, lanes_b, groups, per)),
        [],
        ins,
        [whole(v.shape) for v in ins],
        [shape(jnp.bfloat16, rows, lat_width)],
    )
    return attended.reshape(own_heads, tokens, lat_width)


def solution(mesh):
    in_specs = (
        P(None, "req", None),
        P(None, "req"),
        P(("req", "ctx"), None, None),
        P(("req", "ctx"), None, None),
        P("req", None),
        P("req", None),
        P("req", None),
    )
    out_specs = P("ctx", "req", None)
    return jax.shard_map(shards, mesh=mesh, in_specs=in_specs, out_specs=out_specs, check_vma=False)
```
